32 devices in a mesh: kv: 4 (over z), req: 8 (over y, x, core).
Axes of the slice: x: 2, y: 2, z: 4, core: 2. Of those that a mesh axis runs over, the one named last changes fastest.
Arguments:
- query: bfloat16 [768, 4096], P('req', 'kv'), may hold values from -7 to 7
- latest_key_value: bfloat16 [2, 768, 512], P(None, 'req', 'kv'), may hold values from -5 to 5
- cache: bfloat16 [2, 393216, 512], P(None, 'req', 'kv'), may hold values from -6 to 6
- out_weight: bfloat16 [4096, 4096], P('kv'), may hold values from -0.5 to 0.5
- home: int32 [768], replicated, may hold values from 0 to 767, as said below
- pieces: int32 [2, 768], replicated, may hold values from 0 to 767, as said below
- lengths: int32 [768], replicated, may hold values from 1 to 1920, as said below
Outputs:
- projected: bfloat16 [768, 4096], P('req', 'kv')
The draws below stay inside these ranges and needn't reach their ends.
Inputs may be any that keep to these rules, and one draw needn't show every extreme that they name: A permutation of the home slots; slot g lies on owner g // 96. The requests i * 96 to (i + 1) * 96 - 1 have their homes on exactly 4 owners, exactly 24 on each. `pieces`: guest slot j lies on owner j // 96. The requests of each index of req have exactly 24 guest slots on each of 4 owners; a request has 4 guest slots or none. Every guest slot has 1 to 384 positions. `lengths`: every home slot gets 1 or more positions, and on every owner the slots take exactly 384 pages.
All inputs are finite; a program needn't handle non-finite values.
Results may differ from the reference program's by a relative error of at most 0.0055.
Values may be sent and summed in bfloat16 or wider, within the bound.
A program may use at most 192 MiB of HBM per device.

```python
import jax
import jax.numpy as jnp
from jax import lax

D = 4096
QUERY_HEADS = 32
KEY_VALUE_HEADS = 4
HEAD_WIDTH = 128
REQ_DEV = 96
SPLIT = 4
PAGE_POSITIONS = 128
EXTRA_DEV = 96
OWNER_PAGES = 384
REQUEST_TOTAL = 768
PIECES = 768
HOME_CAP = 24
PIECE_CAP = 24
TOKEN_TOTAL = 393216
N_REQ = 8


def owner_perms(key, length):

    def shuffle_one(subkey):
        return jax.random.permutation(subkey, length)
    return jax.vmap(shuffle_one)(jax.random.split(key, N_REQ)).astype(jnp.int32)


def pair_pages(count):
    list_index = jnp.arange(count, dtype=jnp.int32)
    pair_index = list_index // 2 % 3
    return jnp.where(list_index % 2 == 0, 1 + pair_index, 3 - pair_index).astype(jnp.int32)


def integer_tables(key):
    base_key = jax.random.fold_in(key, 7001)
    subkeys = jax.random.split(base_key, 11)
    device_ids = jnp.arange(N_REQ, dtype=jnp.int32)
    half_count = N_REQ // 2
    home_shift = jax.random.permutation(subkeys[0], N_REQ).astype(jnp.int32)[:half_count]
    piece_shift = jax.random.permutation(subkeys[1], N_REQ).astype(jnp.int32)[:half_count]
    send_order = owner_perms(subkeys[2], REQ_DEV)
    land_order = owner_perms(subkeys[3], REQ_DEV)
    home_group = send_order // HOME_CAP
    home_dest = (device_ids[:, None] + home_shift[home_group]) % N_REQ
    home_slot = land_order[home_dest, send_order]
    home = (home_dest * REQ_DEV + home_slot).reshape(REQUEST_TOTAL).astype(jnp.int32)
    long_count = EXTRA_DEV // SPLIT
    long_order = owner_perms(subkeys[4], REQ_DEV - 1)
    long_pick = jnp.concatenate([jnp.full((N_REQ, 1), REQ_DEV - 1, jnp.int32), long_order[:, :long_count - 1]], axis=1)
    piece_order = owner_perms(subkeys[5], EXTRA_DEV)
    guest_order = owner_perms(subkeys[6], EXTRA_DEV)
    position = jnp.broadcast_to(jnp.arange(EXTRA_DEV, dtype=jnp.int32)[None, :], (N_REQ, EXTRA_DEV))
    piece_group = position // PIECE_CAP
    piece_owner = (device_ids[:, None] + piece_shift[piece_group]) % N_REQ
    long_local = jnp.take_along_axis(long_pick, piece_order % long_count, axis=1)
    piece_request = device_ids[:, None] * REQ_DEV + long_local
    guest_slot = piece_owner * EXTRA_DEV + guest_order[piece_owner, position]
    request_of_slot = jnp.zeros((PIECES,), jnp.int32).at[guest_slot.reshape(-1)].set(piece_request.reshape(-1))
    list_index = jnp.arange(REQ_DEV, dtype=jnp.int32)
    page_list = pair_pages(REQ_DEV)
    count_perm = owner_perms(subkeys[7], REQ_DEV)
    target = home[REQUEST_TOTAL - 1]
    target_owner = target // REQ_DEV
    target_slot = target % REQ_DEV
    target_row = count_perm[target_owner]
    full_at = jnp.argmax((target_row == 1).astype(jnp.int32)).astype(jnp.int32)
    held = target_row[target_slot]
    new_row = jnp.where(list_index == target_slot, 1, jnp.where(list_index == full_at, held, target_row))
    count_perm = count_perm.at[target_owner].set(new_row.astype(jnp.int32))
    home_pages = page_list[count_perm]
    home_tail = jax.random.randint(subkeys[8], (N_REQ, REQ_DEV), 1, PAGE_POSITIONS + 1)
    home_tail = jnp.where(count_perm == 1, PAGE_POSITIONS, home_tail)
    home_slot_len = ((home_pages - 1) * PAGE_POSITIONS + home_tail).astype(jnp.int32)
    guest_list = pair_pages(EXTRA_DEV)
    guest_desc = (-jnp.sort(-guest_list)).astype(jnp.int32)
    is_target = request_of_slot.reshape(N_REQ, EXTRA_DEV) == REQUEST_TOTAL - 1
    guest_perm = owner_perms(subkeys[10], EXTRA_DEV)
    guest_score = jnp.where(is_target, position, EXTRA_DEV + guest_perm).astype(jnp.int32)
    guest_sorted = jnp.argsort(guest_score, axis=1).astype(jnp.int32)
    guest_rank = jnp.argsort(guest_sorted, axis=1).astype(jnp.int32)
    guest_pages = guest_desc[guest_rank]
    guest_tail = jax.random.randint(subkeys[9], (N_REQ, EXTRA_DEV), 1, PAGE_POSITIONS + 1)
    guest_tail = jnp.where(is_target, PAGE_POSITIONS, guest_tail)
    guest_slot_len = ((guest_pages - 1) * PAGE_POSITIONS + guest_tail).astype(jnp.int32)
    home_len = home_slot_len.reshape(REQUEST_TOTAL)
    guest_len = guest_slot_len.reshape(PIECES)
    guest_total = jnp.zeros((REQUEST_TOTAL,), jnp.int32).at[request_of_slot].add(guest_len)
    lengths = (home_len[home] + guest_total).astype(jnp.int32)
    pieces = jnp.stack([request_of_slot, guest_len]).astype(jnp.int32)
    return (home, pieces, lengths)


def draw_home(key, part):
    return integer_tables(key)[0]


def draw_pieces(key, part):
    return integer_tables(key)[1]


def draw_lengths(key, part):
    return integer_tables(key)[2]


def latest_pair(key):
    pair_random_key = jax.random.fold_in(key, 8201)
    return jax.random.truncated_normal(pair_random_key, -5.0, 5.0, (2, REQUEST_TOTAL, KEY_VALUE_HEADS * HEAD_WIDTH), jnp.float32)


def draw_latest_key_value(key, part):
    return latest_pair(key).astype(jnp.bfloat16)


def draw_query(key, part):
    group_width = QUERY_HEADS // KEY_VALUE_HEADS
    self_key = latest_pair(key)[0].reshape(REQUEST_TOTAL, KEY_VALUE_HEADS, 1, HEAD_WIDTH)
    random_key = jax.random.fold_in(key, 8301)
    random_part = jax.random.truncated_normal(random_key, -5.0, 5.0, (REQUEST_TOTAL, KEY_VALUE_HEADS, group_width, HEAD_WIDTH), jnp.float32)
    query_mix = random_part + 0.35 * self_key
    return query_mix.reshape(REQUEST_TOTAL, QUERY_HEADS * HEAD_WIDTH).astype(jnp.bfloat16)


def draw_cache(key, part):
    tensor_shape = (2, TOKEN_TOTAL, KEY_VALUE_HEADS, HEAD_WIDTH)
    random_key = jax.random.fold_in(key, 8501)
    filled_rows = jax.random.truncated_normal(random_key, -5.0, 5.0, tensor_shape, jnp.float32)
    return filled_rows.reshape(2, TOKEN_TOTAL, KEY_VALUE_HEADS * HEAD_WIDTH).astype(jnp.bfloat16)


def steps_of(own_key, dims, cuts, low, top_value):
    def one(dim, parts):
        steps = jax.random.uniform(jax.random.fold_in(jax.random.fold_in(own_key, 6), dim), (parts,), jnp.float32, low / len(cuts), top_value / len(cuts))
        return jnp.repeat(jnp.exp(steps), dims[dim] // parts).reshape((-1,) + (1,) * (len(dims) - dim - 1))

    factor_of = one(*cuts[0])
    for cut in cuts[1:]:
        factor_of = factor_of * one(*cut)
    return factor_of


def gaussian(key, dims, spread, reach, cuts=(), kind=jnp.bfloat16):
    loudness = steps_of(key, dims, cuts, -0.22, 0.18) if cuts else 1.0
    array = jax.random.normal(key, dims, jnp.float32) * spread * loudness
    return jnp.minimum(jnp.maximum(array, -reach), reach).astype(kind)


def setup_inputs(seed: int = 0) -> dict:
    key_list = jax.random.split(jax.random.key(seed), 8)
    query = draw_query(jax.random.fold_in(key_list[7], 71), 0)
    latest_key_value = draw_latest_key_value(jax.random.fold_in(key_list[7], 71), 0)
    cache = draw_cache(jax.random.fold_in(key_list[7], 71), 0)
    out_weight = gaussian(key_list[3], (QUERY_HEADS * HEAD_WIDTH, D), HEAD_WIDTH ** -0.5, 0.5, ((0, 4),))
    home = draw_home(jax.random.fold_in(key_list[7], 71), 0)
    pieces = draw_pieces(jax.random.fold_in(key_list[7], 71), 0)
    lengths = draw_lengths(jax.random.fold_in(key_list[7], 71), 0)
    return dict(query=query, latest_key_value=latest_key_value, cache=cache, out_weight=out_weight, home=home, pieces=pieces, lengths=lengths)


def slot_pages(slot_len, page_count):
    slot_count = slot_len.shape[0]
    per_slot = ((slot_len + PAGE_POSITIONS - 1) // PAGE_POSITIONS).astype(jnp.int32)
    slot_end = jnp.cumsum(per_slot).astype(jnp.int32)
    slot_begin = (slot_end - per_slot).astype(jnp.int32)
    page_index = jnp.arange(page_count, dtype=jnp.int32)
    page_slot = jnp.sum((slot_end[None, :] <= page_index[:, None]).astype(jnp.int32), axis=1).astype(jnp.int32)
    slot_hot = jnp.arange(slot_count, dtype=jnp.int32)[:, None] == page_slot[None, :]
    page_begin = jnp.sum(jnp.where(slot_hot, slot_begin[:, None], 0), axis=0).astype(jnp.int32)
    page_length = jnp.sum(jnp.where(slot_hot, slot_len[:, None], 0), axis=0).astype(jnp.int32)
    page_used = jnp.clip(page_length - (page_index - page_begin) * PAGE_POSITIONS, 0, PAGE_POSITIONS).astype(jnp.int32)
    return page_slot, slot_hot, page_used


def reference(query, latest_key_value, cache, out_weight, home, pieces, lengths):
    group_width = QUERY_HEADS // KEY_VALUE_HEADS
    slot_count = REQ_DEV + EXTRA_DEV
    scale_multiplier = HEAD_WIDTH ** -0.5
    batch_index = jnp.arange(REQUEST_TOTAL, dtype=jnp.int32)
    inverse = jnp.zeros((REQUEST_TOTAL,), jnp.int32).at[home].set(batch_index)
    piece_req = pieces[0]
    piece_len = pieces[1]
    guest_total = jnp.zeros((REQUEST_TOTAL,), jnp.int32).at[piece_req].add(piece_len)
    query_complete = query.astype(jnp.float32).reshape(REQUEST_TOTAL, KEY_VALUE_HEADS, group_width, HEAD_WIDTH)
    cached_rows = cache.reshape(2, N_REQ, OWNER_PAGES, PAGE_POSITIONS, KEY_VALUE_HEADS, HEAD_WIDTH)

    def one_owner(owner_index):
        home_rows = lax.dynamic_slice_in_dim(inverse, owner_index * REQ_DEV, REQ_DEV)
        guest_rows = lax.dynamic_slice_in_dim(piece_req, owner_index * EXTRA_DEV, EXTRA_DEV)
        guest_len = lax.dynamic_slice_in_dim(piece_len, owner_index * EXTRA_DEV, EXTRA_DEV)
        slot_rows = jnp.concatenate([home_rows, guest_rows]).astype(jnp.int32)
        home_len = lengths[home_rows] - guest_total[home_rows]
        slot_len = jnp.concatenate([home_len, guest_len]).astype(jnp.int32)
        page_slot, slot_hot, page_used = slot_pages(slot_len, OWNER_PAGES)
        page_query = query_complete[slot_rows[page_slot]]
        page_keys = cached_rows[0, owner_index].astype(jnp.float32)
        page_values = cached_rows[1, owner_index].astype(jnp.float32)
        scores = jnp.einsum("pkgd,ptkd->pkgt", page_query, page_keys) * scale_multiplier
        in_use = (jnp.arange(PAGE_POSITIONS, dtype=jnp.int32)[None, :] < page_used[:, None])[:, None, None, :]
        scores = jnp.where(in_use, scores, -jnp.inf)
        slot_maximum = jax.ops.segment_max(jnp.max(scores, axis=-1), page_slot, num_segments=slot_count)
        weights = jnp.where(in_use, jnp.exp(scores - slot_maximum[page_slot][..., None]), 0.0).astype(jnp.bfloat16)
        weights = lax.optimization_barrier(weights).astype(jnp.float32)
        slot_total_sum = jax.ops.segment_sum(jnp.sum(weights, axis=-1), page_slot, num_segments=slot_count)
        page_out = jnp.einsum("pkgt,ptkd->pkgd", weights, page_values)
        slot_out = jax.ops.segment_sum(page_out, page_slot, num_segments=slot_count)
        slot_average = (slot_out / slot_total_sum[..., None]).astype(jnp.bfloat16)
        slot_average = lax.optimization_barrier(slot_average).astype(jnp.float32)
        return slot_rows, slot_maximum, slot_total_sum, slot_average

    slot_rows, slot_maximum, slot_total_sum, slot_average = lax.map(one_owner, jnp.arange(N_REQ, dtype=jnp.int32))
    slot_rows = slot_rows.reshape(-1)
    slot_maximum = slot_maximum.reshape(-1, KEY_VALUE_HEADS, group_width)
    slot_total_sum = slot_total_sum.reshape(-1, KEY_VALUE_HEADS, group_width)
    slot_average = slot_average.reshape(-1, KEY_VALUE_HEADS, group_width, HEAD_WIDTH)
    latest_keys = latest_key_value[0].astype(jnp.float32).reshape(REQUEST_TOTAL, KEY_VALUE_HEADS, HEAD_WIDTH)
    latest_values = latest_key_value[1].astype(jnp.float32).reshape(REQUEST_TOTAL, KEY_VALUE_HEADS, HEAD_WIDTH)
    self_score = jnp.einsum("iqcu,iqu->iqc", query_complete, latest_keys) * scale_multiplier
    row_top = jnp.maximum(jax.ops.segment_max(slot_maximum, slot_rows, num_segments=REQUEST_TOTAL), self_score)
    factor = jnp.exp(slot_maximum - row_top[slot_rows])
    own_factor = jnp.exp(self_score - row_top)
    slot_coef = slot_total_sum * factor
    denominator = jax.ops.segment_sum(slot_coef, slot_rows, num_segments=REQUEST_TOTAL) + own_factor
    numerator = jax.ops.segment_sum(slot_average * slot_coef[..., None], slot_rows, num_segments=REQUEST_TOTAL)
    numerator = numerator + latest_values[:, :, None, :] * own_factor[..., None]
    attended = (numerator / denominator[..., None]).astype(jnp.bfloat16).reshape(REQUEST_TOTAL, QUERY_HEADS * HEAD_WIDTH)
    return jnp.dot(attended, out_weight, preferred_element_type=jnp.float32).astype(jnp.bfloat16)
```

```python
import functools

import jax
import jax.numpy as jnp
from jax import lax
from jax.experimental import pallas as pl
from jax.experimental.pallas import tpu as pltpu
from jax.sharding import PartitionSpec as P

QUERY_HEADS = 32
KEY_VALUE_HEADS = 4
HEAD_WIDTH = 128
PAGE_POSITIONS = 128
MAX_SLOT_PAGES = 15
GROUP = QUERY_HEADS // KEY_VALUE_HEADS
PAGE_BLOCK = 32
STATS = 128
NT = (((1,), (1,)), ((), ()))
NEG = float("-inf")
MESH = pl.DeviceIdType.MESH


def tables(home, pieces, lengths, me, req_count, rows, extra, page_count):
    home_cap = 2 * rows // req_count
    piece_cap = 2 * extra // req_count
    entries = -(-(home_cap + piece_cap) // 16) * 16
    total = req_count * entries
    i32 = jnp.int32
    batch = home.shape[0]
    dest = home // rows
    request = jnp.arange(batch, dtype=i32)

    def rank(table):
        width = table.shape[1]
        at = jnp.arange(width, dtype=i32)
        earlier = at[None, :] < at[:, None]
        same = table[:, :, None] == table[:, None, :]
        return jnp.sum((same & earlier[None]).astype(i32), axis=2).reshape(-1)

    home_rank = rank(dest.reshape(req_count, rows))
    piece_req, piece_len = pieces[0], pieces[1]
    piece_src = piece_req // rows
    piece_rank = rank(piece_src.reshape(req_count, extra)) + home_cap
    piece_owner = jnp.arange(req_count * extra, dtype=i32) // extra
    entry = jnp.arange(total, dtype=i32)[:, None]
    home_key = jnp.where(request // rows == me, dest * entries + home_rank, -1)
    piece_key = jnp.where(piece_src == me, piece_owner * entries + piece_rank, -1)
    keys = jnp.concatenate([home_key, piece_key])
    key_rows = jnp.concatenate([request, piece_req]) - me * rows + 1
    row_of_entry = jnp.sum(jnp.where(keys[None, :] == entry, key_rows[None, :], 0), axis=1) - 1
    my_slots = me * rows + jnp.arange(rows, dtype=i32)
    hot = home[None, :] == my_slots[:, None]
    at_home = jnp.sum(jnp.where(hot, (request // rows * entries + home_rank)[None, :], 0), axis=1)
    moved = jnp.sum(
        jnp.where(request[:, None] == piece_req[None, :], piece_len[None, :], 0), axis=1
    )
    home_len = jnp.sum(jnp.where(hot, (lengths - moved)[None, :], 0), axis=1)
    guest_at = lax.dynamic_slice_in_dim(piece_src * entries + piece_rank, me * extra, extra)
    guest_len = lax.dynamic_slice_in_dim(piece_len, me * extra, extra)
    slot_at = jnp.concatenate([at_home, guest_at])
    slot_len = jnp.concatenate([home_len, guest_len])
    per_slot = (slot_len + PAGE_POSITIONS - 1) // PAGE_POSITIONS
    slot = jnp.arange(rows + extra, dtype=i32)
    begin = jnp.sum(jnp.where(slot[None, :] < slot[:, None], per_slot[None, :], 0), axis=1)
    page = jnp.arange(page_count, dtype=i32)[:, None]
    held = (begin[None, :] <= page) & (page < (begin + per_slot)[None, :])
    page_at = jnp.sum(jnp.where(held, slot_at[None, :], 0), axis=1)
    left = slot_len[None, :] - (page - begin[None, :]) * PAGE_POSITIONS
    page_used = jnp.sum(jnp.where(held, jnp.clip(left, 0, PAGE_POSITIONS), 0), axis=1)
    page_first = jnp.sum((held & (page == begin[None, :])).astype(i32), axis=1)
    return entries, row_of_entry, page_at, page_used, page_first


def greet(axis, n):
    me = lax.axis_index(axis)
    barrier = pltpu.get_barrier_semaphore()
    for step in range(1, n):
        peer = lax.rem(me + step, n)
        pl.semaphore_signal(barrier, inc=1, device_id={axis: peer}, device_id_type=MESH)
    return barrier


def send_kernel(n, entries, row_ref, query_ref, out_ref, packed, send_sem, recv_sem, own_sem):
    me = lax.axis_index("req")
    barrier = greet("req", n)
    rows = query_ref.shape[0]
    pick = row_ref[...] == lax.broadcasted_iota(jnp.int32, (n * entries, rows), 1)
    pick = jnp.where(pick, 1.0, 0.0).astype(jnp.bfloat16)
    width = query_ref.shape[1]
    packed[...] = (
        jnp.dot(pick, query_ref[...], preferred_element_type=jnp.float32)
        .astype(jnp.bfloat16)
        .reshape(n, entries, width)
    )
    own = pltpu.make_async_copy(packed.at[me], out_ref.at[me], own_sem)
    own.start()
    pl.semaphore_wait(barrier, n - 1)
    copies = []
    for step in range(1, n):
        peer = lax.rem(me + step, n)
        copy = pltpu.make_async_remote_copy(
            src_ref=packed.at[peer],
            dst_ref=out_ref.at[me],
            send_sem=send_sem.at[step],
            recv_sem=recv_sem.at[step],
            device_id={"req": peer},
            device_id_type=MESH,
        )
        copy.start()
        copies.append(copy)
    own.wait()
    for copy in copies:
        copy.wait()


def segment_scan(x, at, lane, width, combine, empty):
    ahead, behind = x, x
    shift = 1
    while shift < MAX_SLOT_PAGES:
        same = (pltpu.roll(at, shift, 1) == at) & (lane >= shift)
        ahead = combine(ahead, jnp.where(same, pltpu.roll(ahead, shift, 1), empty))
        same = (pltpu.roll(at, width - shift, 1) == at) & (lane < width - shift)
        behind = combine(behind, jnp.where(same, pltpu.roll(behind, width - shift, 1), empty))
        shift *= 2
    return ahead, behind


def attention_kernel(
    used_ref, col_ref, row_ref, first_ref, arrived_ref, key_ref, value_ref,
    out_ref, q_buf, o_buf, top_buf, sum_buf,
):
    step = pl.program_id(0)
    pages = col_ref.shape[0]
    total = arrived_ref.shape[0]
    scale = HEAD_WIDTH ** (-0.5)

    @pl.when(step == 0)
    def _():
        hot = col_ref[...] == lax.broadcasted_iota(jnp.int32, (pages, total), 1)
        hot = jnp.where(hot, 1.0, 0.0).astype(jnp.bfloat16)
        for h in range(GROUP):
            q_buf[pl.ds(h, pages, stride=GROUP), :] = jnp.dot(
                hot,
                arrived_ref[:, h * HEAD_WIDTH : (h + 1) * HEAD_WIDTH],
                preferred_element_type=jnp.float32,
            )

    lane = lax.broadcasted_iota(jnp.int32, (GROUP, 128), 1)
    per_chunk = 128 // PAGE_BLOCK
    lane0 = lax.rem(step, per_chunk) * PAGE_BLOCK
    chunk = step // per_chunk
    tops = top_buf[chunk]
    sums = sum_buf[chunk]
    for j in range(PAGE_BLOCK):
        p = step * PAGE_BLOCK + j
        q = q_buf[pl.ds(pl.multiple_of(p * GROUP, GROUP), GROUP), :].astype(jnp.bfloat16)
        keys = key_ref[0, j * PAGE_POSITIONS : (j + 1) * PAGE_POSITIONS, :]
        values = value_ref[0, j * PAGE_POSITIONS : (j + 1) * PAGE_POSITIONS, :]
        s = lax.dot_general(q, keys, NT, preferred_element_type=jnp.float32) * scale
        s = jnp.where(lane < used_ref[p], s, NEG)
        top = jnp.max(s, axis=1, keepdims=True)
        w = jnp.exp(s - top).astype(jnp.bfloat16)
        total_w = jnp.sum(w.astype(jnp.float32), axis=1, keepdims=True)
        o_buf[pl.ds(pl.multiple_of(p * GROUP, GROUP), GROUP), :] = jnp.dot(
            w, values, preferred_element_type=jnp.float32
        )
        mine = lane == lane0 + j
        tops = jnp.where(mine, top, tops)
        sums = jnp.where(mine, total_w, sums)
    top_buf[chunk] = tops
    sum_buf[chunk] = sums

    @pl.when(step == pl.num_programs(0) - 1)
    def _():
        chunks = pages // 128
        top = jnp.concatenate([top_buf[c] for c in range(chunks)], axis=1)
        page_sum = jnp.concatenate([sum_buf[c] for c in range(chunks)], axis=1)
        at = jnp.broadcast_to(row_ref[...], (GROUP, pages))
        where = lax.broadcasted_iota(jnp.int32, (GROUP, pages), 1)
        ahead, behind = segment_scan(top, at, where, pages, jnp.maximum, NEG)
        slot_top = jnp.maximum(ahead, behind)
        factor = jnp.exp(top - slot_top)
        part = page_sum * factor
        ahead, behind = segment_scan(part, at, where, pages, jnp.add, 0.0)
        slot_sum = ahead + behind - part
        slot_sum = jnp.maximum(slot_sum, part)
        lse = slot_top + jnp.log(slot_sum)
        first = first_ref[...].astype(jnp.float32)
        high = lse.astype(jnp.bfloat16).astype(jnp.float32)
        rest = lse - high
        middle = rest.astype(jnp.bfloat16).astype(jnp.float32)
        low = rest - middle
        stacked = jnp.concatenate(
            [
                high * first,
                middle * first,
                low * first,
                factor / slot_sum,
                jnp.zeros((STATS - 4 * GROUP, pages), jnp.float32),
            ],
            axis=0,
        )
        turned = stacked.T
        hot = row_ref[...] == lax.broadcasted_iota(jnp.int32, (total, pages), 0)
        hot = jnp.where(hot, 1.0, 0.0).astype(jnp.bfloat16)
        for h in range(GROUP):
            values = o_buf[pl.ds(h, pages, stride=GROUP), :]
            at_h = 3 * GROUP + h
            values = (values * turned[:, at_h : at_h + 1]).astype(jnp.bfloat16)
            out_ref[:, h * HEAD_WIDTH : (h + 1) * HEAD_WIDTH] = jnp.dot(
                hot, values, preferred_element_type=jnp.float32
            ).astype(jnp.bfloat16)
        column = lax.broadcasted_iota(jnp.int32, (pages, STATS), 1)
        stats = jnp.where(column < 3 * GROUP, turned, 0.0).astype(jnp.bfloat16)
        out_ref[:, GROUP * HEAD_WIDTH :] = jnp.dot(
            hot, stats, preferred_element_type=jnp.float32
        ).astype(jnp.bfloat16)


def finish_kernel(
    n, kv, entries, row_ref, query_ref, latest_ref, slots_ref, weight_ref, out_ref,
    got, weight, attended, partial, parts, send_sem, recv_sem, kv_send, kv_recv, own_sem, w_sem,
):
    me = lax.axis_index("req")
    me_kv = lax.axis_index("kv")
    barrier = greet("req", n)
    greet("kv", kv)
    load = pltpu.make_async_copy(weight_ref, weight, w_sem)
    own = pltpu.make_async_copy(slots_ref.at[me], got.at[me], own_sem)
    own.start()
    pl.semaphore_wait(barrier, n + kv - 2)
    copies = []
    for step in range(1, n):
        peer = lax.rem(me + step, n)
        copy = pltpu.make_async_remote_copy(
            src_ref=slots_ref.at[peer],
            dst_ref=got.at[me],
            send_sem=send_sem.at[step],
            recv_sem=recv_sem.at[step],
            device_id={"req": peer},
            device_id_type=MESH,
        )
        copy.start()
        copies.append(copy)
    load.start()
    rows = query_ref.shape[0]
    total = n * entries
    scale = HEAD_WIDTH ** (-0.5)
    latest_key = latest_ref[0].astype(jnp.float32)
    latest_value = latest_ref[1].astype(jnp.float32)
    mine = row_ref[...] == lax.broadcasted_iota(jnp.int32, (rows, total), 0)
    selfs = []
    for h in range(GROUP):
        q = query_ref[:, h * HEAD_WIDTH : (h + 1) * HEAD_WIDTH].astype(jnp.float32)
        selfs.append(jnp.sum(q * latest_key, axis=1, keepdims=True) * scale)
    own.wait()
    for copy in copies:
        copy.wait()
    width = GROUP * HEAD_WIDTH
    head = lax.broadcasted_iota(jnp.int32, (GROUP, STATS), 0)
    column = lax.broadcasted_iota(jnp.int32, (GROUP, STATS), 1)
    chosen = (column == head) | (column == head + GROUP) | (column == head + 2 * GROUP)
    chosen = jnp.where(chosen, 1.0, 0.0).astype(jnp.bfloat16)
    lse = lax.dot_general(
        chosen,
        got[:, :, width:].reshape(total, STATS),
        NT,
        preferred_element_type=jnp.float32,
    )
    for h in range(GROUP):
        score = jnp.where(mine, lse[h : h + 1, :], NEG)
        top = jnp.maximum(jnp.max(score, axis=1, keepdims=True), selfs[h])
        w = jnp.exp(score - top)
        own_factor = jnp.exp(selfs[h] - top)
        denominator = jnp.sum(w, axis=1, keepdims=True) + own_factor
        w_high = w.astype(jnp.bfloat16)
        w_low = (w - w_high.astype(jnp.float32)).astype(jnp.bfloat16)
        values = got[:, :, h * HEAD_WIDTH : (h + 1) * HEAD_WIDTH].reshape(total, HEAD_WIDTH)
        numerator = (
            jnp.dot(w_high, values, preferred_element_type=jnp.float32)
            + jnp.dot(w_low, values, preferred_element_type=jnp.float32)
            + latest_value * own_factor
        )
        attended[:, h * HEAD_WIDTH : (h + 1) * HEAD_WIDTH] = (numerator / denominator).astype(
            jnp.bfloat16
        )
    load.wait()
    block = weight.shape[1] // kv

    def project(target):
        return jnp.dot(
            attended[...],
            weight[:, pl.ds(pl.multiple_of(target * block, block), block)],
            preferred_element_type=jnp.float32,
        )

    copies = []
    for step in range(1, kv):
        peer = lax.rem(me_kv + step, kv)
        partial[step] = project(peer).astype(jnp.bfloat16)
        copy = pltpu.make_async_remote_copy(
            src_ref=partial.at[step],
            dst_ref=parts.at[step],
            send_sem=kv_send.at[step],
            recv_sem=kv_recv.at[step],
            device_id={"kv": peer},
            device_id_type=MESH,
        )
        copy.start()
        copies.append(copy)
    result = project(me_kv)
    for step, copy in enumerate(copies, 1):
        copy.wait()
        result = result + parts[step].astype(jnp.float32)
    out_ref[...] = result.astype(jnp.bfloat16)


def per_device(query, latest_key_value, cache, out_weight, home, pieces, lengths):
    n = lax.axis_size("req")
    kv = lax.axis_size("kv")
    me = lax.axis_index("req")
    rows, width = query.shape
    extra = pieces.shape[1] // n
    page_count = cache.shape[1] // PAGE_POSITIONS
    entries, row_of_entry, page_at, page_used, page_first = tables(
        home, pieces, lengths, me, n, rows, extra, page_count
    )
    total = n * entries
    bf16, f32 = jnp.bfloat16, jnp.float32
    vmem = pl.BlockSpec(memory_space=pltpu.VMEM)
    anywhere = pl.BlockSpec(memory_space=pl.ANY)
    dma = pltpu.SemaphoreType.DMA
    arrived = pl.pallas_call(
        functools.partial(send_kernel, n, entries),
        name="send_queries",
        out_shape=jax.ShapeDtypeStruct((n, entries, width), bf16),
        in_specs=[vmem, vmem],
        out_specs=anywhere,
        scratch_shapes=[pltpu.VMEM((n, entries, width), bf16), dma((n,)), dma((n,)), dma],
        compiler_params=pltpu.CompilerParams(collective_id=0, has_side_effects=True),
    )(row_of_entry.reshape(total, 1), query)

    block = PAGE_BLOCK * PAGE_POSITIONS
    whole = lambda shape: pl.BlockSpec(shape, lambda i, used: (0,) * len(shape))
    slots = pl.pallas_call(
        attention_kernel,
        name="attend_pages",
        out_shape=jax.ShapeDtypeStruct((total, width + STATS), bf16),
        grid_spec=pltpu.PrefetchScalarGridSpec(
            num_scalar_prefetch=1,
            grid=(page_count // PAGE_BLOCK,),
            in_specs=[
                whole((page_count, 1)),
                whole((1, page_count)),
                whole((1, page_count)),
                whole((total, width)),
                pl.BlockSpec((1, block, HEAD_WIDTH), lambda i, used: (0, i, 0)),
                pl.BlockSpec((1, block, HEAD_WIDTH), lambda i, used: (1, i, 0)),
            ],
            out_specs=whole((total, width + STATS)),
            scratch_shapes=[
                pltpu.VMEM((page_count * GROUP, HEAD_WIDTH), f32),
                pltpu.VMEM((page_count * GROUP, HEAD_WIDTH), f32),
                pltpu.VMEM((page_count // 128, GROUP, 128), f32),
                pltpu.VMEM((page_count // 128, GROUP, 128), f32),
            ],
        ),
        compiler_params=pltpu.CompilerParams(vmem_limit_bytes=40 << 20),
    )(
        page_used,
        page_at.reshape(page_count, 1),
        page_at.reshape(1, page_count),
        page_first.reshape(1, page_count),
        arrived.reshape(total, width),
        cache,
        cache,
    )

    out_width = out_weight.shape[1] // kv
    return pl.pallas_call(
        functools.partial(finish_kernel, n, kv, entries),
        name="combine_project",
        out_shape=jax.ShapeDtypeStruct((rows, out_width), bf16),
        in_specs=[vmem, vmem, vmem, anywhere, anywhere],
        out_specs=vmem,
        scratch_shapes=[
            pltpu.VMEM((n, entries, width + STATS), bf16),
            pltpu.VMEM(out_weight.shape, bf16),
            pltpu.VMEM((rows, width), bf16),
            pltpu.VMEM((kv, rows, out_width), bf16),
            pltpu.VMEM((kv, rows, out_width), bf16),
            dma((n,)),
            dma((n,)),
            dma((kv,)),
            dma((kv,)),
            dma,
            dma,
        ],
        compiler_params=pltpu.CompilerParams(
            collective_id=1, has_side_effects=True, vmem_limit_bytes=40 << 20
        ),
    )(
        row_of_entry.reshape(1, total),
        query,
        latest_key_value,
        slots.reshape(n, entries, width + STATS),
        out_weight,
    )


def solution(mesh):
    placed = (
        P("req", "kv"),
        P(None, "req", "kv"),
        P(None, "req", "kv"),
        P("kv", None),
        P(),
        P(),
        P(),
    )
    return jax.shard_map(
        per_device, mesh=mesh, in_specs=placed, out_specs=P("req", "kv"), check_vma=False
    )
```

```python
import functools

import jax
import jax.numpy as jnp
from jax import lax
from jax.experimental import pallas as pl
from jax.experimental.pallas import tpu as pltpu
from jax.sharding import PartitionSpec as P

QUERY_HEADS = 32
KEY_VALUE_HEADS = 4
HEAD_WIDTH = 128
PAGE_POSITIONS = 128
MAX_SLOT_PAGES = 15
GROUP = QUERY_HEADS // KEY_VALUE_HEADS
PAGE_BLOCK = 32
STATS = 128
NT = (((1,), (1,)), ((), ()))
NEG = float("-inf")
MESH = pl.DeviceIdType.MESH


def tables(home, pieces, lengths, me, req_count, rows, extra, page_count):
    home_cap = 2 * rows // req_count
    piece_cap = 2 * extra // req_count
    entries = -(-(home_cap + piece_cap) // 16) * 16
    total = req_count * entries
    i32 = jnp.int32
    batch = home.shape[0]
    dest = home // rows
    request = jnp.arange(batch, dtype=i32)

    def rank(table):
        width = table.shape[1]
        at = jnp.arange(width, dtype=i32)
        earlier = at[None, :] < at[:, None]
        same = table[:, :, None] == table[:, None, :]
        return jnp.sum((same & earlier[None]).astype(i32), axis=2).reshape(-1)

    home_rank = rank(dest.reshape(req_count, rows))
    piece_req, piece_len = pieces[0], pieces[1]
    piece_src = piece_req // rows
    piece_rank = rank(piece_src.reshape(req_count, extra)) + home_cap
    piece_owner = jnp.arange(req_count * extra, dtype=i32) // extra
    entry = jnp.arange(total, dtype=i32)[:, None]
    home_key = jnp.where(request // rows == me, dest * entries + home_rank, -1)
    piece_key = jnp.where(piece_src == me, piece_owner * entries + piece_rank, -1)
    keys = jnp.concatenate([home_key, piece_key])
    key_rows = jnp.concatenate([request, piece_req]) - me * rows + 1
    row_of_entry = jnp.sum(jnp.where(keys[None, :] == entry, key_rows[None, :], 0), axis=1) - 1
    my_slots = me * rows + jnp.arange(rows, dtype=i32)
    hot = home[None, :] == my_slots[:, None]
    at_home = jnp.sum(jnp.where(hot, (request // rows * entries + home_rank)[None, :], 0), axis=1)
    moved = jnp.sum(
        jnp.where(request[:, None] == piece_req[None, :], piece_len[None, :], 0), axis=1
    )
    home_len = jnp.sum(jnp.where(hot, (lengths - moved)[None, :], 0), axis=1)
    guest_at = lax.dynamic_slice_in_dim(piece_src * entries + piece_rank, me * extra, extra)
    guest_len = lax.dynamic_slice_in_dim(piece_len, me * extra, extra)
    slot_at = jnp.concatenate([at_home, guest_at])
    slot_len = jnp.concatenate([home_len, guest_len])
    per_slot = (slot_len + PAGE_POSITIONS - 1) // PAGE_POSITIONS
    slot = jnp.arange(rows + extra, dtype=i32)
    begin = jnp.sum(jnp.where(slot[None, :] < slot[:, None], per_slot[None, :], 0), axis=1)
    page = jnp.arange(page_count, dtype=i32)[:, None]
    held = (begin[None, :] <= page) & (page < (begin + per_slot)[None, :])
    page_at = jnp.sum(jnp.where(held, slot_at[None, :], 0), axis=1)
    left = slot_len[None, :] - (page - begin[None, :]) * PAGE_POSITIONS
    page_used = jnp.sum(jnp.where(held, jnp.clip(left, 0, PAGE_POSITIONS), 0), axis=1)
    page_first = jnp.sum((held & (page == begin[None, :])).astype(i32), axis=1)
    return entries, row_of_entry, page_at, page_used, page_first


def greet(axis, n):
    me = lax.axis_index(axis)
    barrier = pltpu.get_barrier_semaphore()
    for step in range(1, n):
        peer = lax.rem(me + step, n)
        pl.semaphore_signal(barrier, inc=1, device_id={axis: peer}, device_id_type=MESH)
    return barrier


def send_kernel(n, entries, row_ref, query_ref, out_ref, packed, send_sem, recv_sem, own_sem):
    me = lax.axis_index("req")
    barrier = greet("req", n)
    rows = query_ref.shape[0]
    pick = row_ref[...] == lax.broadcasted_iota(jnp.int32, (n * entries, rows), 1)
    pick = jnp.where(pick, 1.0, 0.0).astype(jnp.bfloat16)
    width = query_ref.shape[1]
    packed[...] = (
        jnp.dot(pick, query_ref[...], preferred_element_type=jnp.float32)
        .astype(jnp.bfloat16)
        .reshape(n, entries, width)
    )
    own = pltpu.make_async_copy(packed.at[me], out_ref.at[me], own_sem)
    own.start()
    pl.semaphore_wait(barrier, n - 1)
    copies = []
    for step in range(1, n):
        peer = lax.rem(me + step, n)
        copy = pltpu.make_async_remote_copy(
            src_ref=packed.at[peer],
            dst_ref=out_ref.at[me],
            send_sem=send_sem.at[step],
            recv_sem=recv_sem.at[step],
            device_id={"req": peer},
            device_id_type=MESH,
        )
        copy.start()
        copies.append(copy)
    own.wait()
    for copy in copies:
        copy.wait()


def segment_scan(x, at, lane, width, combine, empty):
    ahead, behind = x, x
    shift = 1
    while shift < MAX_SLOT_PAGES:
        same = (pltpu.roll(at, shift, 1) == at) & (lane >= shift)
        ahead = combine(ahead, jnp.where(same, pltpu.roll(ahead, shift, 1), empty))
        same = (pltpu.roll(at, width - shift, 1) == at) & (lane < width - shift)
        behind = combine(behind, jnp.where(same, pltpu.roll(behind, width - shift, 1), empty))
        shift *= 2
    return ahead, behind


def attention_kernel(
    used_ref, col_ref, row_ref, first_ref, arrived_ref, key_ref, value_ref,
    out_ref, q_buf, o_buf, top_buf, sum_buf,
):
    step = pl.program_id(0)
    pages = col_ref.shape[0]
    total = arrived_ref.shape[0]
    scale = HEAD_WIDTH ** (-0.5)

    @pl.when(step == 0)
    def _():
        hot = col_ref[...] == lax.broadcasted_iota(jnp.int32, (pages, total), 1)
        hot = jnp.where(hot, 1.0, 0.0).astype(jnp.bfloat16)
        for h in range(GROUP):
            q_buf[pl.ds(h, pages, stride=GROUP), :] = jnp.dot(
                hot,
                arrived_ref[:, h * HEAD_WIDTH : (h + 1) * HEAD_WIDTH],
                preferred_element_type=jnp.float32,
            )

    lane = lax.broadcasted_iota(jnp.int32, (GROUP, 128), 1)
    pair = (2 * GROUP, 2 * PAGE_POSITIONS)
    column = lax.broadcasted_iota(jnp.int32, pair, 1)
    upper = lax.broadcasted_iota(jnp.int32, pair, 0) < GROUP
    column = jnp.where(upper, column, column - PAGE_POSITIONS)
    column = jnp.where(column < 0, 2 * PAGE_POSITIONS, column)
    per_chunk = 128 // PAGE_BLOCK
    lane0 = lax.rem(step, per_chunk) * PAGE_BLOCK
    chunk = step // per_chunk
    tops = top_buf[chunk]
    sums = sum_buf[chunk]
    row0 = pl.multiple_of(step * (PAGE_BLOCK * GROUP), PAGE_BLOCK * GROUP)
    batch = PAGE_BLOCK // 2
    scores = []
    for j in range(batch):
        q = q_buf[pl.ds(row0 + j * 2 * GROUP, 2 * GROUP), :].astype(jnp.bfloat16)
        keys = key_ref[0, j * 2 * PAGE_POSITIONS : (j + 1) * 2 * PAGE_POSITIONS, :]
        scores.append(lax.dot_general(q, keys, NT, preferred_element_type=jnp.float32))
    weights = []
    for j in range(batch):
        p = step * PAGE_BLOCK + 2 * j
        in_use = column < jnp.where(upper, used_ref[p], used_ref[p + 1])
        s = jnp.where(in_use, scores[j] * scale, NEG)
        top = jnp.max(s, axis=1, keepdims=True)
        w = jnp.exp(s - top).astype(jnp.bfloat16)
        total_w = jnp.sum(w.astype(jnp.float32), axis=1, keepdims=True)
        weights.append(w)
        for k in range(2):
            mine = lane == lane0 + 2 * j + k
            tops = jnp.where(mine, top[k * GROUP : (k + 1) * GROUP], tops)
            sums = jnp.where(mine, total_w[k * GROUP : (k + 1) * GROUP], sums)
    results = []
    for j in range(batch):
        values = value_ref[0, j * 2 * PAGE_POSITIONS : (j + 1) * 2 * PAGE_POSITIONS, :]
        results.append(jnp.dot(weights[j], values, preferred_element_type=jnp.float32))
    for j in range(batch):
        o_buf[pl.ds(row0 + j * 2 * GROUP, 2 * GROUP), :] = results[j]
    top_buf[chunk] = tops
    sum_buf[chunk] = sums

    @pl.when(step == pl.num_programs(0) - 1)
    def _():
        chunks = pages // 128
        top = jnp.concatenate([top_buf[c] for c in range(chunks)], axis=1)
        page_sum = jnp.concatenate([sum_buf[c] for c in range(chunks)], axis=1)
        at = jnp.broadcast_to(row_ref[...], (GROUP, pages))
        where = lax.broadcasted_iota(jnp.int32, (GROUP, pages), 1)
        ahead, behind = segment_scan(top, at, where, pages, jnp.maximum, NEG)
        slot_top = jnp.maximum(ahead, behind)
        factor = jnp.exp(top - slot_top)
        part = page_sum * factor
        ahead, behind = segment_scan(part, at, where, pages, jnp.add, 0.0)
        slot_sum = ahead + behind - part
        slot_sum = jnp.maximum(slot_sum, part)
        lse = slot_top + jnp.log(slot_sum)
        first = first_ref[...].astype(jnp.float32)
        high = lse.astype(jnp.bfloat16).astype(jnp.float32)
        rest = lse - high
        middle = rest.astype(jnp.bfloat16).astype(jnp.float32)
        low = rest - middle
        stacked = jnp.concatenate(
            [
                high * first,
                middle * first,
                low * first,
                factor / slot_sum,
                jnp.zeros((STATS - 4 * GROUP, pages), jnp.float32),
            ],
            axis=0,
        )
        turned = stacked.T
        hot = row_ref[...] == lax.broadcasted_iota(jnp.int32, (total, pages), 0)
        hot = jnp.where(hot, 1.0, 0.0).astype(jnp.bfloat16)
        for h in range(GROUP):
            values = o_buf[pl.ds(h, pages, stride=GROUP), :]
            at_h = 3 * GROUP + h
            values = (values * turned[:, at_h : at_h + 1]).astype(jnp.bfloat16)
            out_ref[:, h * HEAD_WIDTH : (h + 1) * HEAD_WIDTH] = jnp.dot(
                hot, values, preferred_element_type=jnp.float32
            ).astype(jnp.bfloat16)
        column = lax.broadcasted_iota(jnp.int32, (pages, STATS), 1)
        stats = jnp.where(column < 3 * GROUP, turned, 0.0).astype(jnp.bfloat16)
        out_ref[:, GROUP * HEAD_WIDTH :] = jnp.dot(
            hot, stats, preferred_element_type=jnp.float32
        ).astype(jnp.bfloat16)


def finish_kernel(
    n, kv, entries, row_ref, query_ref, latest_ref, slots_ref, weight_ref, out_ref,
    got, weight, attended, partial, parts, send_sem, recv_sem, kv_send, kv_recv, own_sem, w_sem,
):
    me = lax.axis_index("req")
    me_kv = lax.axis_index("kv")
    barrier = greet("req", n)
    greet("kv", kv)
    load = pltpu.make_async_copy(weight_ref, weight, w_sem)
    own = pltpu.make_async_copy(slots_ref.at[me], got.at[me], own_sem)
    own.start()
    pl.semaphore_wait(barrier, n + kv - 2)
    copies = []
    for step in range(1, n):
        peer = lax.rem(me + step, n)
        copy = pltpu.make_async_remote_copy(
            src_ref=slots_ref.at[peer],
            dst_ref=got.at[me],
            send_sem=send_sem.at[step],
            recv_sem=recv_sem.at[step],
            device_id={"req": peer},
            device_id_type=MESH,
        )
        copy.start()
        copies.append(copy)
    load.start()
    rows = query_ref.shape[0]
    total = n * entries
    scale = HEAD_WIDTH ** (-0.5)
    latest_key = latest_ref[0].astype(jnp.float32)
    latest_value = latest_ref[1].astype(jnp.float32)
    mine = row_ref[...] == lax.broadcasted_iota(jnp.int32, (rows, total), 0)
    selfs = []
    for h in range(GROUP):
        q = query_ref[:, h * HEAD_WIDTH : (h + 1) * HEAD_WIDTH].astype(jnp.float32)
        selfs.append(jnp.sum(q * latest_key, axis=1, keepdims=True) * scale)
    own.wait()
    for copy in copies:
        copy.wait()
    width = GROUP * HEAD_WIDTH
    head = lax.broadcasted_iota(jnp.int32, (GROUP, STATS), 0)
    column = lax.broadcasted_iota(jnp.int32, (GROUP, STATS), 1)
    chosen = (column == head) | (column == head + GROUP) | (column == head + 2 * GROUP)
    chosen = jnp.where(chosen, 1.0, 0.0).astype(jnp.bfloat16)
    lse = lax.dot_general(
        chosen,
        got[:, :, width:].reshape(total, STATS),
        NT,
        preferred_element_type=jnp.float32,
    )
    for h in range(GROUP):
        score = jnp.where(mine, lse[h : h + 1, :], NEG)
        top = jnp.maximum(jnp.max(score, axis=1, keepdims=True), selfs[h])
        w = jnp.exp(score - top)
        own_factor = jnp.exp(selfs[h] - top)
        denominator = jnp.sum(w, axis=1, keepdims=True) + own_factor
        w_high = w.astype(jnp.bfloat16)
        w_low = (w - w_high.astype(jnp.float32)).astype(jnp.bfloat16)
        values = got[:, :, h * HEAD_WIDTH : (h + 1) * HEAD_WIDTH].reshape(total, HEAD_WIDTH)
        numerator = (
            jnp.dot(w_high, values, preferred_element_type=jnp.float32)
            + jnp.dot(w_low, values, preferred_element_type=jnp.float32)
            + latest_value * own_factor
        )
        attended[:, h * HEAD_WIDTH : (h + 1) * HEAD_WIDTH] = (numerator / denominator).astype(
            jnp.bfloat16
        )
    load.wait()
    block = weight.shape[1] // kv

    def project(target):
        return jnp.dot(
            attended[...],
            weight[:, pl.ds(pl.multiple_of(target * block, block), block)],
            preferred_element_type=jnp.float32,
        )

    copies = []
    for step in range(1, kv):
        peer = lax.rem(me_kv + step, kv)
        partial[step] = project(peer).astype(jnp.bfloat16)
        copy = pltpu.make_async_remote_copy(
            src_ref=partial.at[step],
            dst_ref=parts.at[step],
            send_sem=kv_send.at[step],
            recv_sem=kv_recv.at[step],
            device_id={"kv": peer},
            device_id_type=MESH,
        )
        copy.start()
        copies.append(copy)
    result = project(me_kv)
    for step, copy in enumerate(copies, 1):
        copy.wait()
        result = result + parts[step].astype(jnp.float32)
    out_ref[...] = result.astype(jnp.bfloat16)


def per_device(query, latest_key_value, cache, out_weight, home, pieces, lengths):
    n = lax.axis_size("req")
    kv = lax.axis_size("kv")
    me = lax.axis_index("req")
    rows, width = query.shape
    extra = pieces.shape[1] // n
    page_count = cache.shape[1] // PAGE_POSITIONS
    entries, row_of_entry, page_at, page_used, page_first = tables(
        home, pieces, lengths, me, n, rows, extra, page_count
    )
    total = n * entries
    bf16, f32 = jnp.bfloat16, jnp.float32
    vmem = pl.BlockSpec(memory_space=pltpu.VMEM)
    anywhere = pl.BlockSpec(memory_space=pl.ANY)
    dma = pltpu.SemaphoreType.DMA
    arrived = pl.pallas_call(
        functools.partial(send_kernel, n, entries),
        name="send_queries",
        out_shape=jax.ShapeDtypeStruct((n, entries, width), bf16),
        in_specs=[vmem, vmem],
        out_specs=anywhere,
        scratch_shapes=[pltpu.VMEM((n, entries, width), bf16), dma((n,)), dma((n,)), dma],
        compiler_params=pltpu.CompilerParams(collective_id=0, has_side_effects=True),
    )(row_of_entry.reshape(total, 1), query)

    block = PAGE_BLOCK * PAGE_POSITIONS
    whole = lambda shape: pl.BlockSpec(shape, lambda i, used: (0,) * len(shape))
    slots = pl.pallas_call(
        attention_kernel,
        name="attend_pages",
        out_shape=jax.ShapeDtypeStruct((total, width + STATS), bf16),
        grid_spec=pltpu.PrefetchScalarGridSpec(
            num_scalar_prefetch=1,
            grid=(page_count // PAGE_BLOCK,),
            in_specs=[
                whole((page_count, 1)),
                whole((1, page_count)),
                whole((1, page_count)),
                whole((total, width)),
                pl.BlockSpec((1, block, HEAD_WIDTH), lambda i, used: (0, i, 0)),
                pl.BlockSpec((1, block, HEAD_WIDTH), lambda i, used: (1, i, 0)),
            ],
            out_specs=whole((total, width + STATS)),
            scratch_shapes=[
                pltpu.VMEM((page_count * GROUP, HEAD_WIDTH), f32),
                pltpu.VMEM((page_count * GROUP, HEAD_WIDTH), f32),
                pltpu.VMEM((page_count // 128, GROUP, 128), f32),
                pltpu.VMEM((page_count // 128, GROUP, 128), f32),
            ],
        ),
        compiler_params=pltpu.CompilerParams(vmem_limit_bytes=56 << 20),
    )(
        page_used,
        page_at.reshape(page_count, 1),
        page_at.reshape(1, page_count),
        page_first.reshape(1, page_count),
        arrived.reshape(total, width),
        cache,
        cache,
    )

    out_width = out_weight.shape[1] // kv
    return pl.pallas_call(
        functools.partial(finish_kernel, n, kv, entries),
        name="combine_project",
        out_shape=jax.ShapeDtypeStruct((rows, out_width), bf16),
        in_specs=[vmem, vmem, vmem, anywhere, anywhere],
        out_specs=vmem,
        scratch_shapes=[
            pltpu.VMEM((n, entries, width + STATS), bf16),
            pltpu.VMEM(out_weight.shape, bf16),
            pltpu.VMEM((rows, width), bf16),
            pltpu.VMEM((kv, rows, out_width), bf16),
            pltpu.VMEM((kv, rows, out_width), bf16),
            dma((n,)),
            dma((n,)),
            dma((kv,)),
            dma((kv,)),
            dma,
            dma,
        ],
        compiler_params=pltpu.CompilerParams(
            collective_id=1, has_side_effects=True, vmem_limit_bytes=56 << 20
        ),
    )(
        row_of_entry.reshape(1, total),
        query,
        latest_key_value,
        slots.reshape(n, entries, width + STATS),
        out_weight,
    )


def solution(mesh):
    placed = (
        P("req", "kv"),
        P(None, "req", "kv"),
        P(None, "req", "kv"),
        P("kv", None),
        P(),
        P(),
        P(),
    )
    return jax.shard_map(
        per_device, mesh=mesh, in_specs=placed, out_specs=P("req", "kv"), check_vma=False
    )
```

```python
import functools

import jax
import jax.numpy as jnp
from jax import lax
from jax.experimental import pallas as pl
from jax.experimental.pallas import tpu as pltpu
from jax.sharding import PartitionSpec as P

QUERY_HEADS = 32
KEY_VALUE_HEADS = 4
HEAD_WIDTH = 128
PAGE_POSITIONS = 128
MAX_SLOT_PAGES = 15
GROUP = QUERY_HEADS // KEY_VALUE_HEADS
PAGE_BLOCK = 32
STATS = 128
NT = (((1,), (1,)), ((), ()))
NEG = float("-inf")
MESH = pl.DeviceIdType.MESH


def tables(home, pieces, lengths, me, req_count, rows, extra, page_count):
    home_cap = 2 * rows // req_count
    piece_cap = 2 * extra // req_count
    entries = -(-(home_cap + piece_cap) // 16) * 16
    total = req_count * entries
    i32 = jnp.int32
    batch = home.shape[0]
    dest = home // rows
    request = jnp.arange(batch, dtype=i32)

    def rank(table):
        width = table.shape[1]
        at = jnp.arange(width, dtype=i32)
        earlier = at[None, :] < at[:, None]
        same = table[:, :, None] == table[:, None, :]
        return jnp.sum((same & earlier[None]).astype(i32), axis=2).reshape(-1)

    home_rank = rank(dest.reshape(req_count, rows))
    piece_req, piece_len = pieces[0], pieces[1]
    piece_src = piece_req // rows
    piece_rank = rank(piece_src.reshape(req_count, extra)) + home_cap
    piece_owner = jnp.arange(req_count * extra, dtype=i32) // extra
    entry = jnp.arange(total, dtype=i32)[:, None]
    home_key = jnp.where(request // rows == me, dest * entries + home_rank, -1)
    piece_key = jnp.where(piece_src == me, piece_owner * entries + piece_rank, -1)
    keys = jnp.concatenate([home_key, piece_key])
    key_rows = jnp.concatenate([request, piece_req]) - me * rows + 1
    row_of_entry = jnp.sum(jnp.where(keys[None, :] == entry, key_rows[None, :], 0), axis=1) - 1
    my_slots = me * rows + jnp.arange(rows, dtype=i32)
    hot = home[None, :] == my_slots[:, None]
    at_home = jnp.sum(jnp.where(hot, (request // rows * entries + home_rank)[None, :], 0), axis=1)
    home_request = jnp.sum(jnp.where(hot, request[None, :], 0), axis=1)
    moved = jnp.sum(
        jnp.where(request[:, None] == piece_req[None, :], piece_len[None, :], 0), axis=1
    )
    home_len = jnp.sum(jnp.where(hot, (lengths - moved)[None, :], 0), axis=1)
    guest_at = lax.dynamic_slice_in_dim(piece_src * entries + piece_rank, me * extra, extra)
    guest_len = lax.dynamic_slice_in_dim(piece_len, me * extra, extra)
    guest_request = lax.dynamic_slice_in_dim(piece_req, me * extra, extra)
    slot_request = jnp.concatenate([home_request, guest_request])
    slot_row = jnp.bitwise_xor(slot_request // rows, me) * rows + slot_request % rows
    slot_at = jnp.concatenate([at_home, guest_at])
    slot_len = jnp.concatenate([home_len, guest_len])
    per_slot = (slot_len + PAGE_POSITIONS - 1) // PAGE_POSITIONS
    slot = jnp.arange(rows + extra, dtype=i32)
    begin = jnp.sum(jnp.where(slot[None, :] < slot[:, None], per_slot[None, :], 0), axis=1)
    page = jnp.arange(page_count, dtype=i32)[:, None]
    held = (begin[None, :] <= page) & (page < (begin + per_slot)[None, :])
    page_at = jnp.sum(jnp.where(held, slot_at[None, :], 0), axis=1)
    page_row = jnp.sum(jnp.where(held, slot_row[None, :], 0), axis=1)
    left = slot_len[None, :] - (page - begin[None, :]) * PAGE_POSITIONS
    page_used = jnp.sum(jnp.where(held, jnp.clip(left, 0, PAGE_POSITIONS), 0), axis=1)
    page_first = jnp.sum((held & (page == begin[None, :])).astype(i32), axis=1)
    return entries, row_of_entry, page_at, page_row, page_used, page_first


def greet(axis, n):
    me = lax.axis_index(axis)
    barrier = pltpu.get_barrier_semaphore()
    for step in range(1, n):
        peer = lax.rem(me + step, n)
        pl.semaphore_signal(barrier, inc=1, device_id={axis: peer}, device_id_type=MESH)
    return barrier


def spread_queries(query, n):
    def swap(block, k):
        return lax.ppermute(block, "req", [(i, i ^ k) for i in range(n)])

    blocks = [query] + [swap(query, k) for k in range(2, n, 2)]
    handed = [swap(block, 1) for block in blocks]
    return [block for both in zip(blocks, handed) for block in both]


def segment_scan(x, at, lane, width, combine, empty):
    ahead, behind = x, x
    shift = 1
    while shift < MAX_SLOT_PAGES:
        same = (pltpu.roll(at, shift, 1) == at) & (lane >= shift)
        ahead = combine(ahead, jnp.where(same, pltpu.roll(ahead, shift, 1), empty))
        same = (pltpu.roll(at, width - shift, 1) == at) & (lane < width - shift)
        behind = combine(behind, jnp.where(same, pltpu.roll(behind, width - shift, 1), empty))
        shift *= 2
    return ahead, behind


def attention_kernel(
    used_ref, col_ref, row_ref, first_ref, *refs
):
    (*block_refs, key_ref, value_ref, out_ref, q_all, q_buf, o_buf, top_buf, sum_buf) = refs
    step = pl.program_id(0)
    pages = col_ref.shape[0]
    total = out_ref.shape[0]
    requests, rows = q_all.shape[0], block_refs[0].shape[0]
    scale = HEAD_WIDTH ** (-0.5)

    @pl.when(step == 0)
    def _():
        for k, block_ref in enumerate(block_refs):
            q_all[k * rows : (k + 1) * rows, :] = block_ref[...]
        hot = col_ref[...] == lax.broadcasted_iota(jnp.int32, (pages, requests), 1)
        hot = jnp.where(hot, 1.0, 0.0).astype(jnp.bfloat16)
        for h in range(GROUP):
            q_buf[pl.ds(h, pages, stride=GROUP), :] = jnp.dot(
                hot,
                q_all[:, h * HEAD_WIDTH : (h + 1) * HEAD_WIDTH],
                preferred_element_type=jnp.float32,
            )

    lane = lax.broadcasted_iota(jnp.int32, (GROUP, 128), 1)
    pair = (2 * GROUP, 2 * PAGE_POSITIONS)
    column = lax.broadcasted_iota(jnp.int32, pair, 1)
    upper = lax.broadcasted_iota(jnp.int32, pair, 0) < GROUP
    column = jnp.where(upper, column, column - PAGE_POSITIONS)
    column = jnp.where(column < 0, 2 * PAGE_POSITIONS, column)
    per_chunk = 128 // PAGE_BLOCK
    lane0 = lax.rem(step, per_chunk) * PAGE_BLOCK
    chunk = step // per_chunk
    tops = top_buf[chunk]
    sums = sum_buf[chunk]
    row0 = pl.multiple_of(step * (PAGE_BLOCK * GROUP), PAGE_BLOCK * GROUP)
    batch = PAGE_BLOCK // 2
    scores = []
    for j in range(batch):
        q = q_buf[pl.ds(row0 + j * 2 * GROUP, 2 * GROUP), :].astype(jnp.bfloat16)
        keys = key_ref[0, j * 2 * PAGE_POSITIONS : (j + 1) * 2 * PAGE_POSITIONS, :]
        scores.append(lax.dot_general(q, keys, NT, preferred_element_type=jnp.float32))
    weights = []
    for j in range(batch):
        p = step * PAGE_BLOCK + 2 * j
        in_use = column < jnp.where(upper, used_ref[p], used_ref[p + 1])
        s = jnp.where(in_use, scores[j] * scale, NEG)
        top = jnp.max(s, axis=1, keepdims=True)
        w = jnp.exp(s - top).astype(jnp.bfloat16)
        weights.append(w)
        for k in range(2):
            mine = lane == lane0 + 2 * j + k
            tops = jnp.where(mine, top[k * GROUP : (k + 1) * GROUP], tops)
    ones = jnp.ones((2 * PAGE_POSITIONS, 128), jnp.bfloat16)
    totals = jnp.dot(
        jnp.concatenate(weights, axis=0), ones, preferred_element_type=jnp.float32
    )
    for p in range(PAGE_BLOCK):
        sums = jnp.where(lane == lane0 + p, totals[p * GROUP : (p + 1) * GROUP], sums)
    results = []
    for j in range(batch):
        values = value_ref[0, j * 2 * PAGE_POSITIONS : (j + 1) * 2 * PAGE_POSITIONS, :]
        results.append(jnp.dot(weights[j], values, preferred_element_type=jnp.float32))
    for j in range(batch):
        o_buf[pl.ds(row0 + j * 2 * GROUP, 2 * GROUP), :] = results[j]
    top_buf[chunk] = tops
    sum_buf[chunk] = sums

    @pl.when(step == pl.num_programs(0) - 1)
    def _():
        chunks = pages // 128
        top = jnp.concatenate([top_buf[c] for c in range(chunks)], axis=1)
        page_sum = jnp.concatenate([sum_buf[c] for c in range(chunks)], axis=1)
        at = jnp.broadcast_to(row_ref[...], (GROUP, pages))
        where = lax.broadcasted_iota(jnp.int32, (GROUP, pages), 1)
        ahead, behind = segment_scan(top, at, where, pages, jnp.maximum, NEG)
        slot_top = jnp.maximum(ahead, behind)
        factor = jnp.exp(top - slot_top)
        part = page_sum * factor
        ahead, behind = segment_scan(part, at, where, pages, jnp.add, 0.0)
        slot_sum = ahead + behind - part
        slot_sum = jnp.maximum(slot_sum, part)
        lse = slot_top + jnp.log(slot_sum)
        first = first_ref[...].astype(jnp.float32)
        high = lse.astype(jnp.bfloat16).astype(jnp.float32)
        rest = lse - high
        middle = rest.astype(jnp.bfloat16).astype(jnp.float32)
        low = rest - middle
        stacked = jnp.concatenate(
            [
                high * first,
                middle * first,
                low * first,
                factor / slot_sum,
                jnp.zeros((STATS - 4 * GROUP, pages), jnp.float32),
            ],
            axis=0,
        )
        turned = stacked.T
        hot = row_ref[...] == lax.broadcasted_iota(jnp.int32, (total, pages), 0)
        hot = jnp.where(hot, 1.0, 0.0).astype(jnp.bfloat16)
        for h in range(GROUP):
            values = o_buf[pl.ds(h, pages, stride=GROUP), :]
            at_h = 3 * GROUP + h
            values = (values * turned[:, at_h : at_h + 1]).astype(jnp.bfloat16)
            out_ref[:, h * HEAD_WIDTH : (h + 1) * HEAD_WIDTH] = jnp.dot(
                hot, values, preferred_element_type=jnp.float32
            ).astype(jnp.bfloat16)
        column = lax.broadcasted_iota(jnp.int32, (pages, STATS), 1)
        stats = jnp.where(column < 3 * GROUP, turned, 0.0).astype(jnp.bfloat16)
        out_ref[:, GROUP * HEAD_WIDTH :] = jnp.dot(
            hot, stats, preferred_element_type=jnp.float32
        ).astype(jnp.bfloat16)


def finish_kernel(
    n, kv, entries, row_ref, query_ref, latest_ref, slots_ref, weight_ref, out_ref,
    got, weight, attended, partial, parts, send_sem, recv_sem, kv_send, kv_recv, own_sem, w_sem,
):
    me = lax.axis_index("req")
    me_kv = lax.axis_index("kv")
    barrier = greet("req", n)
    greet("kv", kv)
    load = pltpu.make_async_copy(weight_ref, weight, w_sem)
    own = pltpu.make_async_copy(slots_ref.at[me], got.at[me], own_sem)
    own.start()
    pl.semaphore_wait(barrier, n + kv - 2)
    copies = []
    for step in range(1, n):
        peer = lax.rem(me + step, n)
        copy = pltpu.make_async_remote_copy(
            src_ref=slots_ref.at[peer],
            dst_ref=got.at[me],
            send_sem=send_sem.at[step],
            recv_sem=recv_sem.at[step],
            device_id={"req": peer},
            device_id_type=MESH,
        )
        copy.start()
        copies.append(copy)
    load.start()
    rows = query_ref.shape[0]
    total = n * entries
    scale = HEAD_WIDTH ** (-0.5)
    latest_key = latest_ref[0].astype(jnp.float32)
    latest_value = latest_ref[1].astype(jnp.float32)
    mine = row_ref[...] == lax.broadcasted_iota(jnp.int32, (rows, total), 0)
    selfs = []
    for h in range(GROUP):
        q = query_ref[:, h * HEAD_WIDTH : (h + 1) * HEAD_WIDTH].astype(jnp.float32)
        selfs.append(jnp.sum(q * latest_key, axis=1, keepdims=True) * scale)
    own.wait()
    for copy in copies:
        copy.wait()
    width = GROUP * HEAD_WIDTH
    head = lax.broadcasted_iota(jnp.int32, (GROUP, STATS), 0)
    column = lax.broadcasted_iota(jnp.int32, (GROUP, STATS), 1)
    chosen = (column == head) | (column == head + GROUP) | (column == head + 2 * GROUP)
    chosen = jnp.where(chosen, 1.0, 0.0).astype(jnp.bfloat16)
    lse = lax.dot_general(
        chosen,
        got[:, :, width:].reshape(total, STATS),
        NT,
        preferred_element_type=jnp.float32,
    )
    for h in range(GROUP):
        score = jnp.where(mine, lse[h : h + 1, :], NEG)
        top = jnp.maximum(jnp.max(score, axis=1, keepdims=True), selfs[h])
        w = jnp.exp(score - top)
        own_factor = jnp.exp(selfs[h] - top)
        denominator = jnp.sum(w, axis=1, keepdims=True) + own_factor
        w_high = w.astype(jnp.bfloat16)
        w_low = (w - w_high.astype(jnp.float32)).astype(jnp.bfloat16)
        values = got[:, :, h * HEAD_WIDTH : (h + 1) * HEAD_WIDTH].reshape(total, HEAD_WIDTH)
        numerator = (
            jnp.dot(w_high, values, preferred_element_type=jnp.float32)
            + jnp.dot(w_low, values, preferred_element_type=jnp.float32)
            + latest_value * own_factor
        )
        attended[:, h * HEAD_WIDTH : (h + 1) * HEAD_WIDTH] = (numerator / denominator).astype(
            jnp.bfloat16
        )
    load.wait()
    block = weight.shape[1] // kv

    def project(target):
        return jnp.dot(
            attended[...],
            weight[:, pl.ds(pl.multiple_of(target * block, block), block)],
            preferred_element_type=jnp.float32,
        )

    copies = []
    for step in range(1, kv):
        peer = lax.rem(me_kv + step, kv)
        partial[step] = project(peer).astype(jnp.bfloat16)
        copy = pltpu.make_async_remote_copy(
            src_ref=partial.at[step],
            dst_ref=parts.at[step],
            send_sem=kv_send.at[step],
            recv_sem=kv_recv.at[step],
            device_id={"kv": peer},
            device_id_type=MESH,
        )
        copy.start()
        copies.append(copy)
    result = project(me_kv)
    for step, copy in enumerate(copies, 1):
        copy.wait()
        result = result + parts[step].astype(jnp.float32)
    out_ref[...] = result.astype(jnp.bfloat16)


def per_device(query, latest_key_value, cache, out_weight, home, pieces, lengths):
    n = lax.axis_size("req")
    kv = lax.axis_size("kv")
    me = lax.axis_index("req")
    rows, width = query.shape
    extra = pieces.shape[1] // n
    page_count = cache.shape[1] // PAGE_POSITIONS
    entries, row_of_entry, page_at, page_row, page_used, page_first = tables(
        home, pieces, lengths, me, n, rows, extra, page_count
    )
    total = n * entries
    bf16, f32 = jnp.bfloat16, jnp.float32
    vmem = pl.BlockSpec(memory_space=pltpu.VMEM)
    anywhere = pl.BlockSpec(memory_space=pl.ANY)
    dma = pltpu.SemaphoreType.DMA
    blocks = spread_queries(query, n)
    block = PAGE_BLOCK * PAGE_POSITIONS
    whole = lambda shape: pl.BlockSpec(shape, lambda i, used: (0,) * len(shape))
    slots = pl.pallas_call(
        attention_kernel,
        name="attend_pages",
        out_shape=jax.ShapeDtypeStruct((total, width + STATS), bf16),
        grid_spec=pltpu.PrefetchScalarGridSpec(
            num_scalar_prefetch=1,
            grid=(page_count // PAGE_BLOCK,),
            in_specs=[
                whole((page_count, 1)),
                whole((1, page_count)),
                whole((1, page_count)),
                *[whole((rows, width))] * n,
                pl.BlockSpec((1, block, HEAD_WIDTH), lambda i, used: (0, i, 0)),
                pl.BlockSpec((1, block, HEAD_WIDTH), lambda i, used: (1, i, 0)),
            ],
            out_specs=whole((total, width + STATS)),
            scratch_shapes=[
                pltpu.VMEM((n * rows, width), bf16),
                pltpu.VMEM((page_count * GROUP, HEAD_WIDTH), f32),
                pltpu.VMEM((page_count * GROUP, HEAD_WIDTH), f32),
                pltpu.VMEM((page_count // 128, GROUP, 128), f32),
                pltpu.VMEM((page_count // 128, GROUP, 128), f32),
            ],
        ),
        compiler_params=pltpu.CompilerParams(vmem_limit_bytes=56 << 20),
    )(
        page_used,
        page_row.reshape(page_count, 1),
        page_at.reshape(1, page_count),
        page_first.reshape(1, page_count),
        *blocks,
        cache,
        cache,
    )

    out_width = out_weight.shape[1] // kv
    return pl.pallas_call(
        functools.partial(finish_kernel, n, kv, entries),
        name="combine_project",
        out_shape=jax.ShapeDtypeStruct((rows, out_width), bf16),
        in_specs=[vmem, vmem, vmem, anywhere, anywhere],
        out_specs=vmem,
        scratch_shapes=[
            pltpu.VMEM((n, entries, width + STATS), bf16),
            pltpu.VMEM(out_weight.shape, bf16),
            pltpu.VMEM((rows, width), bf16),
            pltpu.VMEM((kv, rows, out_width), bf16),
            pltpu.VMEM((kv, rows, out_width), bf16),
            dma((n,)),
            dma((n,)),
            dma((kv,)),
            dma((kv,)),
            dma,
            dma,
        ],
        compiler_params=pltpu.CompilerParams(
            collective_id=1, has_side_effects=True, vmem_limit_bytes=56 << 20
        ),
    )(
        row_of_entry.reshape(1, total),
        query,
        latest_key_value,
        slots.reshape(n, entries, width + STATS),
        out_weight,
    )


def solution(mesh):
    placed = (
        P("req", "kv"),
        P(None, "req", "kv"),
        P(None, "req", "kv"),
        P("kv", None),
        P(),
        P(),
        P(),
    )
    return jax.shard_map(
        per_device, mesh=mesh, in_specs=placed, out_specs=P("req", "kv"), check_vma=False
    )
```

```python
import functools

import jax
import jax.numpy as jnp
from jax import lax
from jax.experimental import pallas as pl
from jax.experimental.pallas import tpu as pltpu
from jax.sharding import PartitionSpec as P

QUERY_HEADS = 32
KEY_VALUE_HEADS = 4
HEAD_WIDTH = 128
PAGE_POSITIONS = 128
MAX_SLOT_PAGES = 15
GROUP = QUERY_HEADS // KEY_VALUE_HEADS
PAGE_BLOCK = 128
STATS = 128
NT = (((1,), (1,)), ((), ()))
NEG = float("-inf")
MESH = pl.DeviceIdType.MESH


def tables(home, pieces, lengths, me, req_count, rows, extra, page_count):
    home_cap = 2 * rows // req_count
    piece_cap = 2 * extra // req_count
    entries = -(-(home_cap + piece_cap) // 16) * 16
    total = req_count * entries
    i32 = jnp.int32
    batch = home.shape[0]
    dest = home // rows
    request = jnp.arange(batch, dtype=i32)

    def rank(table):
        width = table.shape[1]
        at = jnp.arange(width, dtype=i32)
        earlier = at[None, :] < at[:, None]
        same = table[:, :, None] == table[:, None, :]
        return jnp.sum((same & earlier[None]).astype(i32), axis=2).reshape(-1)

    home_rank = rank(dest.reshape(req_count, rows))
    piece_req, piece_len = pieces[0], pieces[1]
    piece_src = piece_req // rows
    piece_rank = rank(piece_src.reshape(req_count, extra)) + home_cap
    piece_owner = jnp.arange(req_count * extra, dtype=i32) // extra
    entry = jnp.arange(total, dtype=i32)[:, None]
    home_key = jnp.where(request // rows == me, dest * entries + home_rank, -1)
    piece_key = jnp.where(piece_src == me, piece_owner * entries + piece_rank, -1)
    keys = jnp.concatenate([home_key, piece_key])
    key_rows = jnp.concatenate([request, piece_req]) - me * rows + 1
    row_of_entry = jnp.sum(jnp.where(keys[None, :] == entry, key_rows[None, :], 0), axis=1) - 1
    my_slots = me * rows + jnp.arange(rows, dtype=i32)
    hot = home[None, :] == my_slots[:, None]
    at_home = jnp.sum(jnp.where(hot, (request // rows * entries + home_rank)[None, :], 0), axis=1)
    home_request = jnp.sum(jnp.where(hot, request[None, :], 0), axis=1)
    moved = jnp.sum(
        jnp.where(request[:, None] == piece_req[None, :], piece_len[None, :], 0), axis=1
    )
    home_len = jnp.sum(jnp.where(hot, (lengths - moved)[None, :], 0), axis=1)
    guest_at = lax.dynamic_slice_in_dim(piece_src * entries + piece_rank, me * extra, extra)
    guest_len = lax.dynamic_slice_in_dim(piece_len, me * extra, extra)
    guest_request = lax.dynamic_slice_in_dim(piece_req, me * extra, extra)
    slot_request = jnp.concatenate([home_request, guest_request])
    slot_row = jnp.bitwise_xor(slot_request // rows, me) * rows + slot_request % rows
    slot_at = jnp.concatenate([at_home, guest_at])
    slot_len = jnp.concatenate([home_len, guest_len])
    per_slot = (slot_len + PAGE_POSITIONS - 1) // PAGE_POSITIONS
    slot = jnp.arange(rows + extra, dtype=i32)
    begin = jnp.sum(jnp.where(slot[None, :] < slot[:, None], per_slot[None, :], 0), axis=1)
    page = jnp.arange(page_count, dtype=i32)[:, None]
    held = (begin[None, :] <= page) & (page < (begin + per_slot)[None, :])
    page_at = jnp.sum(jnp.where(held, slot_at[None, :], 0), axis=1)
    page_row = jnp.sum(jnp.where(held, slot_row[None, :], 0), axis=1)
    left = slot_len[None, :] - (page - begin[None, :]) * PAGE_POSITIONS
    page_used = jnp.sum(jnp.where(held, jnp.clip(left, 0, PAGE_POSITIONS), 0), axis=1)
    page_first = jnp.sum((held & (page == begin[None, :])).astype(i32), axis=1)
    return entries, row_of_entry, page_at, page_row, page_used, page_first


def greet(axis, n):
    me = lax.axis_index(axis)
    barrier = pltpu.get_barrier_semaphore()
    for step in range(1, n):
        peer = lax.rem(me + step, n)
        pl.semaphore_signal(barrier, inc=1, device_id={axis: peer}, device_id_type=MESH)
    return barrier


def spread_queries(query, n):
    def swap(block, k):
        return lax.ppermute(block, "req", [(i, i ^ k) for i in range(n)])

    blocks = [query] + [swap(query, k) for k in range(2, n, 2)]
    handed = [swap(block, 1) for block in blocks]
    return [block for both in zip(blocks, handed) for block in both]


def segment_scan(x, at, lane, width, combine, empty):
    ahead, behind = x, x
    shift = 1
    while shift < MAX_SLOT_PAGES:
        same = (pltpu.roll(at, shift, 1) == at) & (lane >= shift)
        ahead = combine(ahead, jnp.where(same, pltpu.roll(ahead, shift, 1), empty))
        same = (pltpu.roll(at, width - shift, 1) == at) & (lane < width - shift)
        behind = combine(behind, jnp.where(same, pltpu.roll(behind, width - shift, 1), empty))
        shift *= 2
    return ahead, behind


def attention_kernel(
    used_ref, col_ref, row_ref, first_ref, *refs
):
    (*block_refs, key_ref, value_ref, out_ref, q_all, q_buf, o_buf, top_buf, sum_buf) = refs
    step = pl.program_id(0)
    pages = col_ref.shape[0]
    total = out_ref.shape[0]
    requests, rows = q_all.shape[0], block_refs[0].shape[0]
    scale = HEAD_WIDTH ** (-0.5)

    @pl.when(step == 0)
    def _():
        for k, block_ref in enumerate(block_refs):
            q_all[k * rows : (k + 1) * rows, :] = block_ref[...]
        hot = col_ref[...] == lax.broadcasted_iota(jnp.int32, (pages, requests), 1)
        hot = jnp.where(hot, 1.0, 0.0).astype(jnp.bfloat16)
        for h in range(GROUP):
            q_buf[pl.ds(h, pages, stride=GROUP), :] = jnp.dot(
                hot,
                q_all[:, h * HEAD_WIDTH : (h + 1) * HEAD_WIDTH],
                preferred_element_type=jnp.float32,
            )

    lane = lax.broadcasted_iota(jnp.int32, (GROUP, 128), 1)
    pair = (2 * GROUP, 2 * PAGE_POSITIONS)
    column = lax.broadcasted_iota(jnp.int32, pair, 1)
    upper = lax.broadcasted_iota(jnp.int32, pair, 0) < GROUP
    column = jnp.where(upper, column, column - PAGE_POSITIONS)
    column = jnp.where(column < 0, 2 * PAGE_POSITIONS, column)
    per_chunk = 128 // PAGE_BLOCK
    lane0 = lax.rem(step, per_chunk) * PAGE_BLOCK
    chunk = step // per_chunk
    tops = top_buf[chunk]
    sums = sum_buf[chunk]
    row0 = pl.multiple_of(step * (PAGE_BLOCK * GROUP), PAGE_BLOCK * GROUP)
    batch = PAGE_BLOCK // 2
    scores = []
    for j in range(batch):
        q = q_buf[pl.ds(row0 + j * 2 * GROUP, 2 * GROUP), :].astype(jnp.bfloat16)
        keys = key_ref[0, j * 2 * PAGE_POSITIONS : (j + 1) * 2 * PAGE_POSITIONS, :]
        scores.append(lax.dot_general(q, keys, NT, preferred_element_type=jnp.float32))
    weights = []
    for j in range(batch):
        p = step * PAGE_BLOCK + 2 * j
        in_use = column < jnp.where(upper, used_ref[p], used_ref[p + 1])
        s = jnp.where(in_use, scores[j] * scale, NEG)
        top = jnp.max(s, axis=1, keepdims=True)
        w = jnp.exp(s - top).astype(jnp.bfloat16)
        weights.append(w)
        for k in range(2):
            mine = lane == lane0 + 2 * j + k
            tops = jnp.where(mine, top[k * GROUP : (k + 1) * GROUP], tops)
    ones = jnp.ones((2 * PAGE_POSITIONS, 128), jnp.bfloat16)
    totals = jnp.dot(
        jnp.concatenate(weights, axis=0), ones, preferred_element_type=jnp.float32
    )
    for p in range(PAGE_BLOCK):
        sums = jnp.where(lane == lane0 + p, totals[p * GROUP : (p + 1) * GROUP], sums)
    results = []
    for j in range(batch):
        values = value_ref[0, j * 2 * PAGE_POSITIONS : (j + 1) * 2 * PAGE_POSITIONS, :]
        results.append(jnp.dot(weights[j], values, preferred_element_type=jnp.float32))
    for j in range(batch):
        o_buf[pl.ds(row0 + j * 2 * GROUP, 2 * GROUP), :] = results[j]
    top_buf[chunk] = tops
    sum_buf[chunk] = sums

    @pl.when(step == pl.num_programs(0) - 1)
    def _():
        chunks = pages // 128
        top = jnp.concatenate([top_buf[c] for c in range(chunks)], axis=1)
        page_sum = jnp.concatenate([sum_buf[c] for c in range(chunks)], axis=1)
        at = jnp.broadcast_to(row_ref[...], (GROUP, pages))
        where = lax.broadcasted_iota(jnp.int32, (GROUP, pages), 1)
        ahead, behind = segment_scan(top, at, where, pages, jnp.maximum, NEG)
        slot_top = jnp.maximum(ahead, behind)
        factor = jnp.exp(top - slot_top)
        part = page_sum * factor
        ahead, behind = segment_scan(part, at, where, pages, jnp.add, 0.0)
        slot_sum = ahead + behind - part
        slot_sum = jnp.maximum(slot_sum, part)
        lse = slot_top + jnp.log(slot_sum)
        first = first_ref[...].astype(jnp.float32)
        high = lse.astype(jnp.bfloat16).astype(jnp.float32)
        rest = lse - high
        middle = rest.astype(jnp.bfloat16).astype(jnp.float32)
        low = rest - middle
        stacked = jnp.concatenate(
            [
                high * first,
                middle * first,
                low * first,
                factor / slot_sum,
                jnp.zeros((STATS - 4 * GROUP, pages), jnp.float32),
            ],
            axis=0,
        )
        turned = stacked.T
        hot = row_ref[...] == lax.broadcasted_iota(jnp.int32, (total, pages), 0)
        hot = jnp.where(hot, 1.0, 0.0).astype(jnp.bfloat16)
        for h in range(GROUP):
            values = o_buf[pl.ds(h, pages, stride=GROUP), :]
            at_h = 3 * GROUP + h
            values = (values * turned[:, at_h : at_h + 1]).astype(jnp.bfloat16)
            out_ref[:, h * HEAD_WIDTH : (h + 1) * HEAD_WIDTH] = jnp.dot(
                hot, values, preferred_element_type=jnp.float32
            ).astype(jnp.bfloat16)
        column = lax.broadcasted_iota(jnp.int32, (pages, STATS), 1)
        stats = jnp.where(column < 3 * GROUP, turned, 0.0).astype(jnp.bfloat16)
        out_ref[:, GROUP * HEAD_WIDTH :] = jnp.dot(
            hot, stats, preferred_element_type=jnp.float32
        ).astype(jnp.bfloat16)


def finish_kernel(
    n, kv, entries, row_ref, query_ref, latest_ref, slots_ref, weight_ref, out_ref,
    got, weight, attended, partial, parts, send_sem, recv_sem, kv_send, kv_recv, own_sem, w_sem,
):
    me = lax.axis_index("req")
    me_kv = lax.axis_index("kv")
    barrier = greet("req", n)
    greet("kv", kv)
    load = pltpu.make_async_copy(weight_ref, weight, w_sem)
    own = pltpu.make_async_copy(slots_ref.at[me], got.at[me], own_sem)
    own.start()
    pl.semaphore_wait(barrier, n + kv - 2)
    copies = []
    for step in range(1, n):
        peer = lax.rem(me + step, n)
        copy = pltpu.make_async_remote_copy(
            src_ref=slots_ref.at[peer],
            dst_ref=got.at[me],
            send_sem=send_sem.at[step],
            recv_sem=recv_sem.at[step],
            device_id={"req": peer},
            device_id_type=MESH,
        )
        copy.start()
        copies.append(copy)
    load.start()
    rows = query_ref.shape[0]
    total = n * entries
    scale = HEAD_WIDTH ** (-0.5)
    latest_key = latest_ref[0].astype(jnp.float32)
    latest_value = latest_ref[1].astype(jnp.float32)
    mine = row_ref[...] == lax.broadcasted_iota(jnp.int32, (rows, total), 0)
    selfs = []
    for h in range(GROUP):
        q = query_ref[:, h * HEAD_WIDTH : (h + 1) * HEAD_WIDTH].astype(jnp.float32)
        selfs.append(jnp.sum(q * latest_key, axis=1, keepdims=True) * scale)
    own.wait()
    for copy in copies:
        copy.wait()
    width = GROUP * HEAD_WIDTH
    head = lax.broadcasted_iota(jnp.int32, (GROUP, STATS), 0)
    column = lax.broadcasted_iota(jnp.int32, (GROUP, STATS), 1)
    chosen = (column == head) | (column == head + GROUP) | (column == head + 2 * GROUP)
    chosen = jnp.where(chosen, 1.0, 0.0).astype(jnp.bfloat16)
    lse = lax.dot_general(
        chosen,
        got[:, :, width:].reshape(total, STATS),
        NT,
        preferred_element_type=jnp.float32,
    )
    for h in range(GROUP):
        score = jnp.where(mine, lse[h : h + 1, :], NEG)
        top = jnp.maximum(jnp.max(score, axis=1, keepdims=True), selfs[h])
        w = jnp.exp(score - top)
        own_factor = jnp.exp(selfs[h] - top)
        denominator = jnp.sum(w, axis=1, keepdims=True) + own_factor
        w_high = w.astype(jnp.bfloat16)
        w_low = (w - w_high.astype(jnp.float32)).astype(jnp.bfloat16)
        values = got[:, :, h * HEAD_WIDTH : (h + 1) * HEAD_WIDTH].reshape(total, HEAD_WIDTH)
        numerator = (
            jnp.dot(w_high, values, preferred_element_type=jnp.float32)
            + jnp.dot(w_low, values, preferred_element_type=jnp.float32)
            + latest_value * own_factor
        )
        attended[:, h * HEAD_WIDTH : (h + 1) * HEAD_WIDTH] = (numerator / denominator).astype(
            jnp.bfloat16
        )
    load.wait()
    block = weight.shape[1] // kv

    def project(target):
        return jnp.dot(
            attended[...],
            weight[:, pl.ds(pl.multiple_of(target * block, block), block)],
            preferred_element_type=jnp.float32,
        )

    copies = []
    order = [*range(kv // 2, kv), *range(1, kv // 2)]
    for step in order:
        peer = me_kv ^ step
        partial[step] = project(peer).astype(jnp.bfloat16)
        copy = pltpu.make_async_remote_copy(
            src_ref=partial.at[step],
            dst_ref=parts.at[step],
            send_sem=kv_send.at[step],
            recv_sem=kv_recv.at[step],
            device_id={"kv": peer},
            device_id_type=MESH,
        )
        copy.start()
        copies.append(copy)
    result = project(me_kv)
    for step, copy in zip(order, copies):
        copy.wait()
        result = result + parts[step].astype(jnp.float32)
    out_ref[...] = result.astype(jnp.bfloat16)


def per_device(query, latest_key_value, cache, out_weight, home, pieces, lengths):
    n = lax.axis_size("req")
    kv = lax.axis_size("kv")
    me = lax.axis_index("req")
    rows, width = query.shape
    extra = pieces.shape[1] // n
    page_count = cache.shape[1] // PAGE_POSITIONS
    entries, row_of_entry, page_at, page_row, page_used, page_first = tables(
        home, pieces, lengths, me, n, rows, extra, page_count
    )
    total = n * entries
    bf16, f32 = jnp.bfloat16, jnp.float32
    vmem = pl.BlockSpec(memory_space=pltpu.VMEM)
    anywhere = pl.BlockSpec(memory_space=pl.ANY)
    dma = pltpu.SemaphoreType.DMA
    blocks = spread_queries(query, n)
    block = PAGE_BLOCK * PAGE_POSITIONS
    whole = lambda shape: pl.BlockSpec(shape, lambda i, used: (0,) * len(shape))
    slots = pl.pallas_call(
        attention_kernel,
        name="attend_pages",
        out_shape=jax.ShapeDtypeStruct((total, width + STATS), bf16),
        grid_spec=pltpu.PrefetchScalarGridSpec(
            num_scalar_prefetch=1,
            grid=(page_count // PAGE_BLOCK,),
            in_specs=[
                whole((page_count, 1)),
                whole((1, page_count)),
                whole((1, page_count)),
                *[whole((rows, width))] * n,
                pl.BlockSpec((1, block, HEAD_WIDTH), lambda i, used: (0, i, 0)),
                pl.BlockSpec((1, block, HEAD_WIDTH), lambda i, used: (1, i, 0)),
            ],
            out_specs=whole((total, width + STATS)),
            scratch_shapes=[
                pltpu.VMEM((n * rows, width), bf16),
                pltpu.VMEM((page_count * GROUP, HEAD_WIDTH), f32),
                pltpu.VMEM((page_count * GROUP, HEAD_WIDTH), f32),
                pltpu.VMEM((page_count // 128, GROUP, 128), f32),
                pltpu.VMEM((page_count // 128, GROUP, 128), f32),
            ],
        ),
        compiler_params=pltpu.CompilerParams(vmem_limit_bytes=56 << 20),
    )(
        page_used,
        page_row.reshape(page_count, 1),
        page_at.reshape(1, page_count),
        page_first.reshape(1, page_count),
        *blocks,
        cache,
        cache,
    )

    out_width = out_weight.shape[1] // kv
    return pl.pallas_call(
        functools.partial(finish_kernel, n, kv, entries),
        name="combine_project",
        out_shape=jax.ShapeDtypeStruct((rows, out_width), bf16),
        in_specs=[vmem, vmem, vmem, anywhere, anywhere],
        out_specs=vmem,
        scratch_shapes=[
            pltpu.VMEM((n, entries, width + STATS), bf16),
            pltpu.VMEM(out_weight.shape, bf16),
            pltpu.VMEM((rows, width), bf16),
            pltpu.VMEM((kv, rows, out_width), bf16),
            pltpu.VMEM((kv, rows, out_width), bf16),
            dma((n,)),
            dma((n,)),
            dma((kv,)),
            dma((kv,)),
            dma,
            dma,
        ],
        compiler_params=pltpu.CompilerParams(
            collective_id=1, has_side_effects=True, vmem_limit_bytes=56 << 20
        ),
    )(
        row_of_entry.reshape(1, total),
        query,
        latest_key_value,
        slots.reshape(n, entries, width + STATS),
        out_weight,
    )


def solution(mesh):
    placed = (
        P("req", "kv"),
        P(None, "req", "kv"),
        P(None, "req", "kv"),
        P("kv", None),
        P(),
        P(),
        P(),
    )
    return jax.shard_map(
        per_device, mesh=mesh, in_specs=placed, out_specs=P("req", "kv"), check_vma=False
    )
```
